32 devices in a mesh: dp: 8 (over y, x, core), expert: 4 (over z).
Axes of the slice: x: 2, y: 2, z: 4, core: 2. Of those that a mesh axis runs over, the one named last changes fastest.
Arguments:
- tokens: bfloat16 [512, 6144], P('dp', 'expert'), may hold values from -6 to 6
- cotangent: bfloat16 [512, 6144], P('dp', 'expert'), may hold values from -6 to 6
- expert_ids: int32 [512, 2], P('dp'), may hold values from 0 to 7, all different within a row; in each aligned block of 64 rows (0 to 63, 64 to 127, ...) at most 48 rows name the same one
- routing_weights: bfloat16 [512, 2], P('dp'), may hold values from 0.099609375 to 0.8984375
- w_gate: bfloat16 [6144, 65536], P(None, ('dp', 'expert')), may hold values from -0.078125 to 0.078125
- w_up: bfloat16 [6144, 65536], P(None, ('dp', 'expert')), may hold values from -0.078125 to 0.078125
- w_down: bfloat16 [65536, 6144], P(('dp', 'expert')), may hold values from -0.0625 to 0.0625
- embedding: bfloat16 [32768, 6144], P(('dp', 'expert')), may hold values from -0.078125 to 0.078125
Outputs:
- input_grad: bfloat16 [512, 6144], P('dp', 'expert')
- scores: float32 [512, 32768], P(None, ('dp', 'expert'))
The draws below stay inside these ranges and needn't reach their ends.
Inputs may be any that keep to these rules, and one draw needn't show every extreme that they name: `expert_ids`: the 2 ids of a token differ. Within the 64 rows of one index of dp no expert is named more than 48 times, a bound that some block reaches.
All inputs are finite; a program needn't handle non-finite values.
Results may differ from the reference program's by a relative error of at most 0.012.
Values may be sent and summed in bfloat16 or wider, within the bound.
A program may use at most 256 MiB of HBM per device.

```python
import math
import jax
import jax.numpy as jnp
import numpy as np
from jax import lax

D = 6144
E = 8
TOP = 2
V = 32768
FF = 8192
TOK_DEV = 64
TOKENS = 512
MOST = 48
OWNERS = 1
COLS = 2048
N_EXPERT = 4


def levels(stream_key, shape, pieces, smallest, largest):
    factor_of, own = 1.0, jax.random.fold_in(stream_key, 6)
    for dim, shards_of in pieces:
        steps = jnp.exp(jax.random.uniform(jax.random.fold_in(own, dim), (shards_of,), jnp.float32, smallest / len(pieces), largest / len(pieces)))
        factor_of = factor_of * jnp.repeat(steps, shape[dim] // shards_of).reshape([-1 if axis == dim else 1 for axis in range(len(shape))])
    return factor_of


def routed_block(rng, own, number, rows, number_of, top, most, slope):
    order = jax.random.permutation(rng, number_of)
    crowded, common = portions_of(number_of, rows * top, most, slope, True), portions_of(number_of, rows * top, most, slope, False)
    places = jnp.arange(number_of)

    def named(sizes, turn):
        used = int((sizes > 0).sum())
        fixed = max(1, used // 4)
        moved = fixed + (places - fixed + turn * (used - fixed)) % max(1, number_of - fixed)
        return jnp.zeros((number_of,), jnp.int32).at[order[jnp.where(places < fixed, places, moved)]].set(jnp.asarray(sizes, jnp.int32))

    sizes = jnp.where(number % 4 == 0, named(crowded, number // 4), named(common, number - number // 4 - 1))
    mixed = jax.random.permutation(jax.random.fold_in(own, 3), number_of)
    source_of, sink = mixed[0:number_of // 2 * 2:2], mixed[1:number_of // 2 * 2:2]
    margin = jnp.minimum(sizes[source_of] - 1, most - sizes[sink]) // 2
    margin = jnp.where((source_of == order[0]) | (sink == order[0]) | (sizes[sink] == 0), 0, jnp.maximum(margin, 0))
    moved = jax.random.randint(jax.random.fold_in(own, 4), (number_of // 2,), 0, 1 << 20) % (margin + 1)
    sizes = sizes.at[source_of].add(-moved).at[sink].add(moved)
    items = jnp.searchsorted(jnp.cumsum(sizes), jnp.arange(rows * top), side="right").astype(jnp.int32)
    grid = items.reshape(top, rows).T
    grid = grid[jax.random.permutation(jax.random.fold_in(own, 1), rows)]
    turn = jax.random.randint(jax.random.fold_in(own, 2), (rows, 1), 0, top)
    return jnp.take_along_axis(grid, (jnp.arange(top)[None, :] + turn) % top, axis=1)


def portions_of(count, total, most, slope, full):
    weights = [(1 << 20) // math.isqrt(standing ** slope) + 1 for standing in range(1, count + 1)]
    largest = most if full else min(most, max(-(-total // count), total * weights[0] // sum(weights)))
    least = 1 if total - largest >= count - 1 else 0
    given, rest = [largest] + [least] * (count - 1), total - largest - least * (count - 1)
    while rest > 0:
        candidates = [i for i in range(1, count) if given[i] < largest] or [i for i in range(1, count) if given[i] < most]
        pool, budget = sum([weights[i] for i in candidates]), rest
        for i in candidates:
            extra = min(most - given[i], max(1, budget * weights[i] // pool), rest)
            given[i] = given[i] + extra
            rest = rest - extra
    return np.array(given)


def bell_draw(rng, dims, width, bound, split=(), kind=jnp.bfloat16):
    gain = levels(rng, dims, split, -0.22, 0.18) if split else 1.0
    drawn = jax.random.normal(rng, dims, jnp.float32) * width * gain
    return jnp.minimum(jnp.maximum(drawn, -bound), bound).astype(kind)


def setup_inputs(seed: int = 0) -> dict:
    key_list = jax.random.split(jax.random.key(seed), 9)
    tokens = bell_draw(key_list[0], (TOKENS, D), 1.0, 6.0, ((0, 8), (1, 4)))
    cotangent = bell_draw(key_list[1], (TOKENS, D), 1.0, 6.0, ((0, 8), (1, 4)))
    expert_ids_keys = jax.random.split(jax.random.fold_in(key_list[2], 1), TOKENS // TOK_DEV)
    expert_ids_turns = jax.random.permutation(jax.random.fold_in(key_list[2], 3), TOKENS // TOK_DEV)
    expert_ids = jax.vmap(lambda own, number: routed_block(jax.random.fold_in(key_list[2], 2), own, number, TOK_DEV, E, TOP, MOST, 2))(expert_ids_keys, expert_ids_turns).reshape((TOKENS, TOP))
    routing_weights = jnp.clip(0.099609375 + 0.7988281 * jax.random.uniform(key_list[3], (TOKENS, TOP), jnp.float32) ** levels(key_list[3], (TOKENS, TOP), ((0, 8),), -0.2, 0.2), 0.099609375, 0.8984375).astype(jnp.bfloat16)
    w_gate = bell_draw(key_list[4], (D, E * FF), D ** -0.5, 0.078125, ((1, 32),))
    w_up = bell_draw(key_list[5], (D, E * FF), D ** -0.5, 0.078125, ((1, 32),))
    w_down = bell_draw(key_list[6], (E * FF, D), FF ** -0.5, 0.0625, ((0, 32),))
    embedding = bell_draw(key_list[7], (V, D), D ** -0.5, 0.078125, ((0, 32),))
    return {"tokens": tokens, "cotangent": cotangent, "expert_ids": expert_ids, "routing_weights": routing_weights, "w_gate": w_gate, "w_up": w_up, "w_down": w_down, "embedding": embedding}


block_rows = 128


def reference(tokens, cotangent, expert_ids, routing_weights, w_gate, w_up, w_down, embedding):
    pair_count = TOKENS * TOP
    flat_ids = expert_ids.reshape(pair_count).astype(jnp.int32)
    expert_iota = jnp.arange(E, dtype=jnp.int32)
    onehot = (flat_ids[:, None] == expert_iota[None, :]).astype(jnp.int32)
    before = jnp.cumsum(onehot, axis=0) - onehot
    slot_rank = jnp.sum(before * onehot, axis=1).astype(jnp.int32)
    loads = jnp.sum(onehot, axis=0)
    padded = ((loads + block_rows - 1) // block_rows) * block_rows
    ends = jnp.cumsum(padded).astype(jnp.int32)
    starts = (ends - padded).astype(jnp.int32)
    position = (jnp.sum(onehot * starts[None, :], axis=1) + slot_rank).astype(jnp.int32)
    block_count = pair_count // block_rows + E + 1
    table = jnp.full((block_count * block_rows,), pair_count, dtype=jnp.int32)
    table = table.at[position].set(jnp.arange(pair_count, dtype=jnp.int32))
    block_start = jnp.arange(block_count, dtype=jnp.int32) * block_rows
    block_expert = jnp.minimum(jnp.sum((ends[None, :] <= block_start[:, None]).astype(jnp.int32), axis=1), E - 1).astype(jnp.int32)
    tokens_pad = jnp.concatenate([tokens, jnp.zeros((1, D), jnp.bfloat16)], axis=0)
    cotangent_pad = jnp.concatenate([cotangent, jnp.zeros((1, D), jnp.bfloat16)], axis=0)
    gates_pad = jnp.concatenate([routing_weights.reshape(pair_count).astype(jnp.float32), jnp.zeros((1,), jnp.float32)])
    token_of = jnp.concatenate([jnp.arange(pair_count, dtype=jnp.int32) // TOP, jnp.array([TOKENS], dtype=jnp.int32)])
    blocks_per_expert = FF // COLS

    def one_block(index):
        pair_ids = lax.dynamic_slice_in_dim(table, (index * block_rows).astype(jnp.int32), block_rows)
        rows = token_of[pair_ids]
        rows_x = tokens_pad[rows]
        rows_dy = cotangent_pad[rows]
        gates = gates_pad[pair_ids][:, None]
        offset = (block_expert[index] * FF).astype(jnp.int32)
        gate_cols = lax.dynamic_slice_in_dim(w_gate, offset, FF, 1)
        up_cols = lax.dynamic_slice_in_dim(w_up, offset, FF, 1)
        down_rows = lax.dynamic_slice_in_dim(w_down, offset, FF, 0)
        gate_pre = jnp.dot(rows_x, gate_cols, preferred_element_type=jnp.float32)
        up_pre = jnp.dot(rows_x, up_cols, preferred_element_type=jnp.float32)
        scaled = gates * jnp.dot(rows_dy, down_rows.T, preferred_element_type=jnp.float32)
        sigma = jax.nn.sigmoid(gate_pre)
        grad_gate = (scaled * up_pre * sigma * (1.0 + gate_pre * (1.0 - sigma))).astype(jnp.bfloat16)
        grad_up = (scaled * gate_pre * sigma).astype(jnp.bfloat16)
        grad_gate3 = grad_gate.astype(jnp.float32).reshape(block_rows, blocks_per_expert, COLS)
        grad_up3 = grad_up.astype(jnp.float32).reshape(block_rows, blocks_per_expert, COLS)
        gate_cols3 = gate_cols.astype(jnp.float32).reshape(D, blocks_per_expert, COLS)
        up_cols3 = up_cols.astype(jnp.float32).reshape(D, blocks_per_expert, COLS)
        block_part = jnp.einsum("rbc,dbc->rbd", grad_gate3, gate_cols3) + jnp.einsum("rbc,dbc->rbd", grad_up3, up_cols3)
        block_part = lax.optimization_barrier(block_part.astype(jnp.bfloat16)).astype(jnp.float32)
        owner_part = jnp.sum(block_part.reshape(block_rows, OWNERS, N_EXPERT, D), axis=2)
        owner_part = lax.optimization_barrier(owner_part.astype(jnp.bfloat16)).astype(jnp.float32)
        return jnp.sum(owner_part, axis=1)

    contributions = lax.map(one_block, jnp.arange(block_count, dtype=jnp.int32))
    token_rows = token_of[table]
    grads = jnp.zeros((TOKENS + 1, D), jnp.float32).at[token_rows].add(contributions.reshape(block_count * block_rows, D))
    input_grad = grads[:TOKENS].astype(jnp.bfloat16)
    scores = -jnp.dot(input_grad, embedding.T, preferred_element_type=jnp.float32)
    return input_grad, scores
```

```python
import functools

import jax
import jax.numpy as jnp
from jax import lax
from jax.experimental import pallas as pl
from jax.experimental.pallas import tpu as pltpu
from jax.sharding import PartitionSpec as P

E = 8
TOP = 2
MOST = 48
MESH = pl.DeviceIdType.MESH
HBM = pl.BlockSpec(memory_space=pl.ANY)
VMEM = pl.BlockSpec(memory_space=pltpu.VMEM)
GRANT = 60 * 1024 * 1024


def places():
    dp = lax.axis_index("dp")
    z = lax.axis_index("expert")
    core = lax.rem(dp, 2)
    x = lax.rem(dp // 2, 2)
    y = dp // 4
    dx = 2 - 4 * x
    dy = 4 - 8 * y
    dc = 1 - 2 * core
    return dp, z, dx, dy, dc


def meet(dp, z, others):
    barrier = pltpu.get_barrier_semaphore()
    for d in others:
        pl.semaphore_signal(barrier, inc=1, device_id=d, device_id_type=MESH)
    pl.semaphore_wait(barrier, len(others))


def gather_kernel(count, with_meta, *refs):
    ins = refs[:count]
    at = count
    if with_meta:
        meta_in = refs[at]
        at += 1
    outs = refs[at : at + count]
    at += count
    if with_meta:
        meta_out = refs[at]
        at += 1
    send, recv, own, msend, mrecv = refs[at:]
    dp, z, dx, dy, dc = places()
    rows, cols = ins[0].shape
    xn, yn, sib = dp + dx, dp + dy, dp + dc
    dg = dp + dx + dy
    zs = [lax.rem(z + d, 4) for d in range(4)]
    dps = [lax.rem(dp + d, 8) for d in range(8)]
    meet(dp, z, [(dp, zs[d]) for d in (1, 2, 3)] + [(dps[d], z) for d in range(1, 8)])

    def block(a, src, q, lo=0, n=rows):
        return outs[a].at[
            pl.ds(pl.multiple_of(src * rows + lo, 16), n), pl.ds(pl.multiple_of(q * cols, 128), cols)
        ]

    def remote(src, dst, i, kind, dev):
        return pltpu.make_async_remote_copy(
            src_ref=src, dst_ref=dst, send_sem=send.at[i, kind], recv_sem=recv.at[i, kind],
            device_id=dev, device_id_type=MESH,
        )

    sent = []

    def go(c):
        c.start()
        sent.append(c)

    local = []
    if with_meta:
        here = pl.ds(pl.multiple_of(dp * rows, 16), rows)
        metas = []
        for d in range(1, 8):
            c = pltpu.make_async_remote_copy(
                src_ref=meta_in, dst_ref=meta_out.at[here, :], send_sem=msend.at[d], recv_sem=mrecv.at[d],
                device_id=(dps[d], z), device_id_type=MESH,
            )
            c.start()
            metas.append(c)
        c = pltpu.make_async_copy(meta_in, meta_out.at[here, :], own.at[count])
        c.start()
        local.append(c)
    half = rows // 2
    for a in range(count):
        c = pltpu.make_async_copy(ins[a], block(a, dp, z), own.at[a])
        c.start()
        local.append(c)

    def q_of(d):
        return lax.rem(z + 4 - d, 4)

    def stage0(i):
        a, d = divmod(i, 4)
        if d == 0:
            for k in (1, 2, 3):
                go(remote(ins[a], block(a, dp, z), a * 4 + k, 0, (dp, zs[k])))
            src = ins[a]
        else:
            q = q_of(d)
            remote(block(a, dp, q), block(a, dp, q), i, 0, (dp, z)).wait_recv()
            src = block(a, dp, q)
        q = q_of(d)
        go(remote(src, block(a, dp, q), i, 1, (xn, z)))
        go(remote(src, block(a, dp, q), i, 2, (yn, z)))
        go(remote(src, block(a, dp, q), i, 5, (sib, z)))

    def stage1(i):
        a, d = divmod(i, 4)
        q = q_of(d)
        b = block(a, xn, q)
        remote(b, b, i, 1, (xn, z)).wait_recv()
        h = block(a, xn, q, 0, half)
        go(remote(h, h, i, 3, (yn, z)))
        go(remote(b, b, i, 6, (sib, z)))
        b = block(a, yn, q)
        remote(b, b, i, 2, (yn, z)).wait_recv()
        h = block(a, yn, q, half, half)
        go(remote(h, h, i, 4, (xn, z)))
        go(remote(b, b, i, 7, (sib, z)))

    def stage2(i):
        a, d = divmod(i, 4)
        q = q_of(d)
        h = block(a, dg, q, 0, half)
        remote(h, h, i, 3, (yn, z)).wait_recv()
        h = block(a, dg, q, half, half)
        remote(h, h, i, 4, (xn, z)).wait_recv()
        b = block(a, dg, q)
        go(remote(b, b, i, 8, (sib, z)))

    total = 4 * count
    for t in range(total + 2):
        if t < total:
            stage0(t)
        if 0 <= t - 1 < total:
            stage1(t - 1)
        if 0 <= t - 2 < total:
            stage2(t - 2)
    for i in range(total):
        a, d = divmod(i, 4)
        q = q_of(d)
        for k, src in ((5, sib), (6, xn + dc), (7, yn + dc), (8, dg + dc)):
            b = block(a, src, q)
            remote(b, b, i, k, (sib, z)).wait_recv()
    if with_meta:
        for d in range(1, 8):
            metas[d - 1].wait()
    for c in local:
        c.wait()
    for c in sent:
        c.wait_send()


def gather(arrays, meta, collective_id):
    count = len(arrays)
    rows, cols = arrays[0].shape
    out = [jax.ShapeDtypeStruct((rows * 8, cols * 4), jnp.bfloat16)] * count
    args = list(arrays)
    if meta is not None:
        args.append(meta)
        out.append(jax.ShapeDtypeStruct((rows * 8, meta.shape[1]), jnp.bfloat16))
    return pl.pallas_call(
        functools.partial(gather_kernel, count, meta is not None),
        out_shape=out,
        in_specs=[VMEM] * len(args),
        out_specs=[HBM] * len(out),
        scratch_shapes=[
            pltpu.SemaphoreType.DMA((4 * count, 9)),
            pltpu.SemaphoreType.DMA((4 * count, 9)),
            pltpu.SemaphoreType.DMA((count + 1,)),
            pltpu.SemaphoreType.DMA((8,)),
            pltpu.SemaphoreType.DMA((8,)),
        ],
        compiler_params=pltpu.CompilerParams(
            collective_id=collective_id, has_side_effects=True, vmem_limit_bytes=GRANT
        ),
    )(*args)


def reduce_kernel(p_ref, out_ref, got_s, got_d, got_x, got_y, got_z, acc, send, recv):
    dp, z, dx, dy, dc = places()
    rows, cols = out_ref.shape
    half = rows // 2
    xn, yn, sib, dg = dp + dx, dp + dy, dp + dc, dp + dx + dy
    zs = [lax.rem(z + d, 4) for d in range(4)]
    meet(dp, z, [(dp, zs[d]) for d in (1, 2, 3)] + [(xn, z), (yn, z), (sib, z)])
    f32 = jnp.float32

    def remote(src, dst, i, kind, dev):
        return pltpu.make_async_remote_copy(
            src_ref=src, dst_ref=dst, send_sem=send.at[i, kind], recv_sem=recv.at[i, kind],
            device_id=dev, device_id_type=MESH,
        )

    sent = []

    def go(c):
        c.start()
        sent.append(c)

    lo, hi = pl.ds(0, half), pl.ds(half, half)
    order = [zs[2], zs[1], zs[3], zs[0]]
    slots = [(3, dg), (1, xn), (2, yn), (0, dp)]
    for i in range(4):
        q = order[i]
        for s, owner in slots:
            go(remote(p_ref.at[q, owner + dc], got_s.at[q, s], i, s, (sib, z)))

    def arrive_s(i, s):
        remote(got_s.at[order[i], s], got_s.at[order[i], s], i, s, (sib, z)).wait_recv()

    def fold_diag(i):
        q = order[i]
        arrive_s(i, 3)
        acc[q, 3] = (p_ref[q, dg].astype(f32) + got_s[q, 3].astype(f32)).astype(jnp.bfloat16)
        go(remote(acc.at[q, 3, lo, :], got_d.at[q, 0], i, 4, (yn, z)))
        go(remote(acc.at[q, 3, hi, :], got_d.at[q, 1], i, 5, (xn, z)))

    def fold_side(i):
        q = order[i]
        arrive_s(i, 1)
        remote(got_d.at[q, 0], got_d.at[q, 0], i, 4, (yn, z)).wait_recv()
        acc[q, 1, lo, :] = (
            p_ref[q, xn, lo, :].astype(f32) + got_s[q, 1, lo, :].astype(f32) + got_d[q, 0].astype(f32)
        ).astype(jnp.bfloat16)
        acc[q, 1, hi, :] = (
            p_ref[q, xn, hi, :].astype(f32) + got_s[q, 1, hi, :].astype(f32)
        ).astype(jnp.bfloat16)
        go(remote(acc.at[q, 1], got_x.at[q], i, 6, (xn, z)))
        arrive_s(i, 2)
        remote(got_d.at[q, 1], got_d.at[q, 1], i, 5, (xn, z)).wait_recv()
        acc[q, 2, hi, :] = (
            p_ref[q, yn, hi, :].astype(f32) + got_s[q, 2, hi, :].astype(f32) + got_d[q, 1].astype(f32)
        ).astype(jnp.bfloat16)
        acc[q, 2, lo, :] = (
            p_ref[q, yn, lo, :].astype(f32) + got_s[q, 2, lo, :].astype(f32)
        ).astype(jnp.bfloat16)
        go(remote(acc.at[q, 2], got_y.at[q], i, 7, (yn, z)))

    def fold_own(i):
        q = order[i]
        arrive_s(i, 0)
        remote(got_x.at[q], got_x.at[q], i, 6, (xn, z)).wait_recv()
        remote(got_y.at[q], got_y.at[q], i, 7, (yn, z)).wait_recv()
        total = (
            p_ref[q, dp].astype(f32) + got_s[q, 0].astype(f32) + got_x[q].astype(f32) + got_y[q].astype(f32)
        )
        if i < 3:
            acc[q, 0] = total.astype(jnp.bfloat16)
            go(remote(acc.at[q, 0], got_z.at[i], i, 8, (dp, q)))
            return None
        for k in range(3):
            remote(got_z.at[k], got_z.at[k], k, 8, (dp, z)).wait_recv()
            total = total + got_z[k].astype(f32)
        out_ref[...] = total.astype(jnp.bfloat16)

    for t in range(6):
        if t < 4:
            fold_diag(t)
        if 0 <= t - 1 < 4:
            fold_side(t - 1)
        if 0 <= t - 2 < 4:
            fold_own(t - 2)
    for c in sent:
        c.wait_send()


def reduce_scatter(dense, rows, cols, collective_id):
    bf = jnp.bfloat16
    return pl.pallas_call(
        reduce_kernel,
        out_shape=jax.ShapeDtypeStruct((rows, cols), bf),
        in_specs=[VMEM],
        out_specs=VMEM,
        scratch_shapes=[
            pltpu.VMEM((4, 4, rows, cols), bf),
            pltpu.VMEM((4, 2, rows // 2, cols), bf),
            pltpu.VMEM((4, rows, cols), bf),
            pltpu.VMEM((4, rows, cols), bf),
            pltpu.VMEM((3, rows, cols), bf),
            pltpu.VMEM((4, 4, rows, cols), bf),
            pltpu.SemaphoreType.DMA((4, 9)),
            pltpu.SemaphoreType.DMA((4, 9)),
        ],
        compiler_params=pltpu.CompilerParams(
            collective_id=collective_id, has_side_effects=True, vmem_limit_bytes=GRANT
        ),
    )(dense)


CONTRACT = (((1,), (1,)), ((), ()))


def expert_rows(flat_x, flat_dy, gates, w_gate, w_up, w_down):
    f32 = jnp.float32
    gate_pre = jnp.dot(flat_x, w_gate, preferred_element_type=f32)
    up_pre = jnp.dot(flat_x, w_up, preferred_element_type=f32)
    scaled = gates * lax.dot_general(flat_dy, w_down, CONTRACT, preferred_element_type=f32)
    sigma = jax.nn.sigmoid(gate_pre)
    grad_gate = (scaled * up_pre * sigma * (1.0 + gate_pre * (1.0 - sigma))).astype(jnp.bfloat16)
    grad_up = (scaled * gate_pre * sigma).astype(jnp.bfloat16)
    part = lax.dot_general(grad_gate, w_gate, CONTRACT, preferred_element_type=f32)
    part = part + lax.dot_general(grad_up, w_up, CONTRACT, preferred_element_type=f32)
    return part.astype(jnp.bfloat16)


def on_device_block(tokens, cotangent, expert_ids, routing_weights, w_gate, w_up, w_down, embedding):
    f32, bf = jnp.float32, jnp.bfloat16
    rows, cols = tokens.shape
    count = rows * 8
    meta = jnp.concatenate(
        [expert_ids.astype(bf), routing_weights, jnp.zeros((rows, 128 - 2 * TOP), bf)], axis=1
    )
    all_x, all_dy, all_meta = gather([tokens, cotangent], meta, 1)
    mine = lax.axis_index("dp").astype(f32)
    named = all_meta[:, :TOP].astype(f32) == mine
    match = jnp.sum(named.astype(f32), axis=1)
    weight = jnp.sum(jnp.where(named, all_meta[:, TOP : 2 * TOP].astype(f32), 0.0), axis=1)
    row = jnp.arange(count, dtype=jnp.int32)
    earlier = (row[None, :] < row[:, None]).astype(bf)
    rank = jnp.dot(earlier, match.astype(bf)[:, None], preferred_element_type=f32)[:, 0].astype(jnp.int32)
    slot = jnp.arange(E * MOST, dtype=jnp.int32)
    chosen = (slot[:, None] == rank[None, :]) & (match[None, :] > 0.5)
    select = chosen.astype(bf)
    gates = jnp.sum(jnp.where(chosen, weight[None, :], 0.0), axis=1, keepdims=True)
    flat_x = jnp.dot(select, all_x, preferred_element_type=f32).astype(bf)
    flat_dy = jnp.dot(select, all_dy, preferred_element_type=f32).astype(bf)
    part = expert_rows(flat_x, flat_dy, gates, w_gate, w_up, w_down)
    dense = lax.dot_general(select, part, (((0,), (0,)), ((), ())), preferred_element_type=f32).astype(bf)
    dense = dense.reshape(8, rows, 4, cols).transpose(2, 0, 1, 3)
    input_grad = reduce_scatter(dense, rows, cols, 2)
    (whole,) = gather([input_grad], None, 3)
    scores = -lax.dot_general(whole, embedding, CONTRACT, preferred_element_type=f32)
    return input_grad, scores


def owner_work(rows_x, rows_dy, gates, w_gate, w_up, w_down):
    sources, slots, width = rows_x.shape
    part = expert_rows(
        rows_x.reshape(sources * slots, width),
        rows_dy.reshape(sources * slots, width),
        gates.reshape(sources * slots, 1).astype(jnp.float32),
        w_gate,
        w_up,
        w_down,
    )
    return part.reshape(sources, slots, width)


def on_device_any(tokens, cotangent, expert_ids, routing_weights, w_gate, w_up, w_down, embedding):
    dp_count = lax.axis_size("dp")
    owners = dp_count // E
    tok_rows = tokens.shape[0]
    pair_count = tok_rows * TOP
    flat_ids = expert_ids.reshape(pair_count)
    expert_iota = jnp.arange(E, dtype=jnp.int32)
    onehot = (flat_ids[:, None] == expert_iota[None, :]).astype(jnp.float32)
    pair_iota = jnp.arange(pair_count, dtype=jnp.int32)
    earlier = (pair_iota[:, None] > pair_iota[None, :]).astype(jnp.float32)
    before = jnp.dot(earlier, onehot, precision=lax.Precision.HIGHEST)
    slot_rank = jnp.sum(before * onehot, axis=1).astype(jnp.int32)
    slot_of = flat_ids * MOST + slot_rank
    slot_iota = jnp.arange(E * MOST, dtype=jnp.int32)
    placed = slot_iota[:, None] == slot_of[None, :]
    flat_weights = routing_weights.reshape(pair_count).astype(jnp.float32)
    gate_slots = jnp.sum(jnp.where(placed, flat_weights[None, :], 0.0), axis=1).astype(jnp.bfloat16)
    select_rows = jnp.sum(
        placed.reshape(E * MOST, tok_rows, TOP).astype(jnp.float32), axis=2
    ).astype(jnp.bfloat16)
    send_gates = jnp.repeat(gate_slots.reshape(E, MOST), owners, axis=0)

    def dispatch(rows):
        packed = jnp.dot(select_rows, rows, preferred_element_type=jnp.float32).astype(jnp.bfloat16)
        return jnp.repeat(packed.reshape(E, MOST, rows.shape[1]), owners, axis=0)

    whole_x, whole_dy = (
        lax.all_gather(tokens, "expert", axis=1, tiled=True),
        lax.all_gather(cotangent, "expert", axis=1, tiled=True),
    )
    recv_x, recv_dy, recv_gates = (
        lax.all_to_all(dispatch(whole_x), "dp", split_axis=0, concat_axis=0, tiled=True),
        lax.all_to_all(dispatch(whole_dy), "dp", split_axis=0, concat_axis=0, tiled=True),
        lax.all_to_all(send_gates, "dp", split_axis=0, concat_axis=0, tiled=True),
    )
    partial_rows = owner_work(recv_x, recv_dy, recv_gates, w_gate, w_up, w_down)
    came_back = lax.all_to_all(partial_rows, "dp", split_axis=0, concat_axis=0, tiled=True)
    returned = lax.psum_scatter(
        came_back.astype(jnp.float32).astype(jnp.bfloat16),
        "expert",
        scatter_dimension=2,
        tiled=True,
    )
    spread = jnp.repeat(select_rows.reshape(E, MOST, tok_rows), owners, axis=0).reshape(
        dp_count * MOST, tok_rows
    )
    feature_count = returned.shape[2]
    input_grad = lax.dot_general(
        spread,
        returned.reshape(dp_count * MOST, feature_count),
        (((0,), (0,)), ((), ())),
        preferred_element_type=jnp.float32,
    ).astype(jnp.bfloat16)
    whole_grad = lax.all_gather(input_grad, "expert", axis=1, tiled=True)
    scores = -lax.dot_general(
        lax.all_gather(whole_grad, "dp", axis=0, tiled=True),
        embedding,
        (((1,), (1,)), ((), ())),
        preferred_element_type=jnp.float32,
    )
    return (input_grad, scores)


def solution(mesh):
    placed = (
        P("dp", "expert"),
        P("dp", "expert"),
        P("dp", None),
        P("dp", None),
        P(None, ("dp", "expert")),
        P(None, ("dp", "expert")),
        P(("dp", "expert"), None),
        P(("dp", "expert"), None),
    )
    block = mesh.shape["dp"] == 8 and mesh.shape["expert"] == 4
    return jax.shard_map(
        on_device_block if block else on_device_any,
        mesh=mesh,
        in_specs=placed,
        out_specs=(P("dp", "expert"), P(None, ("dp", "expert"))),
        check_vma=False,
    )
```

```python
import functools

import jax
import jax.numpy as jnp
from jax import lax
from jax.experimental import pallas as pl
from jax.experimental.pallas import tpu as pltpu
from jax.sharding import PartitionSpec as P

E = 8
TOP = 2
MOST = 48
MESH = pl.DeviceIdType.MESH
HBM = pl.BlockSpec(memory_space=pl.ANY)
VMEM = pl.BlockSpec(memory_space=pltpu.VMEM)
GRANT = 60 * 1024 * 1024


def places():
    dp = lax.axis_index("dp")
    z = lax.axis_index("expert")
    core = lax.rem(dp, 2)
    x = lax.rem(dp // 2, 2)
    y = dp // 4
    dx = 2 - 4 * x
    dy = 4 - 8 * y
    dc = 1 - 2 * core
    return dp, z, dx, dy, dc


def meet(dp, z, others):
    barrier = pltpu.get_barrier_semaphore()
    for d in others:
        pl.semaphore_signal(barrier, inc=1, device_id=d, device_id_type=MESH)
    pl.semaphore_wait(barrier, len(others))


def gather_kernel(count, with_meta, *refs):
    ins = refs[:count]
    at = count
    if with_meta:
        meta_in = refs[at]
        at += 1
    outs = refs[at : at + count]
    at += count
    if with_meta:
        meta_out = refs[at]
        at += 1
    send, recv, own, msend, mrecv = refs[at:]
    dp, z, dx, dy, dc = places()
    rows, cols = ins[0].shape
    xn, yn, sib = dp + dx, dp + dy, dp + dc
    dg = dp + dx + dy
    zs = [lax.rem(z + d, 4) for d in range(4)]
    dps = [lax.rem(dp + d, 8) for d in range(8)]
    meet(dp, z, [(dp, zs[d]) for d in (1, 2, 3)] + [(dps[d], z) for d in range(1, 8)])

    def block(a, src, q, lo=0, n=rows):
        return outs[a].at[
            pl.ds(pl.multiple_of(src * rows + lo, 16), n), pl.ds(pl.multiple_of(q * cols, 128), cols)
        ]

    def remote(src, dst, i, kind, dev):
        return pltpu.make_async_remote_copy(
            src_ref=src, dst_ref=dst, send_sem=send.at[i, kind], recv_sem=recv.at[i, kind],
            device_id=dev, device_id_type=MESH,
        )

    sent = []

    def go(c):
        c.start()
        sent.append(c)

    local = []
    if with_meta:
        here = pl.ds(pl.multiple_of(dp * rows, 16), rows)
        metas = []
        for d in range(1, 8):
            c = pltpu.make_async_remote_copy(
                src_ref=meta_in, dst_ref=meta_out.at[here, :], send_sem=msend.at[d], recv_sem=mrecv.at[d],
                device_id=(dps[d], z), device_id_type=MESH,
            )
            c.start()
            metas.append(c)
        c = pltpu.make_async_copy(meta_in, meta_out.at[here, :], own.at[count])
        c.start()
        local.append(c)
    half = rows // 2
    for a in range(count):
        c = pltpu.make_async_copy(ins[a], block(a, dp, z), own.at[a])
        c.start()
        local.append(c)

    def q_of(d):
        return lax.rem(z + 4 - d, 4)

    def stage0(i):
        a, d = divmod(i, 4)
        if d == 0:
            for k in (1, 2, 3):
                go(remote(ins[a], block(a, dp, z), a * 4 + k, 0, (dp, zs[k])))
            src = ins[a]
        else:
            q = q_of(d)
            remote(block(a, dp, q), block(a, dp, q), i, 0, (dp, z)).wait_recv()
            src = block(a, dp, q)
        q = q_of(d)
        go(remote(src, block(a, dp, q), i, 1, (xn, z)))
        go(remote(src, block(a, dp, q), i, 2, (yn, z)))
        go(remote(src, block(a, dp, q), i, 5, (sib, z)))

    def stage1(i):
        a, d = divmod(i, 4)
        q = q_of(d)
        b = block(a, xn, q)
        remote(b, b, i, 1, (xn, z)).wait_recv()
        h = block(a, xn, q, 0, half)
        go(remote(h, h, i, 3, (yn, z)))
        go(remote(b, b, i, 6, (sib, z)))
        b = block(a, yn, q)
        remote(b, b, i, 2, (yn, z)).wait_recv()
        h = block(a, yn, q, half, half)
        go(remote(h, h, i, 4, (xn, z)))
        go(remote(b, b, i, 7, (sib, z)))

    def stage2(i):
        a, d = divmod(i, 4)
        q = q_of(d)
        h = block(a, dg, q, 0, half)
        remote(h, h, i, 3, (yn, z)).wait_recv()
        h = block(a, dg, q, half, half)
        remote(h, h, i, 4, (xn, z)).wait_recv()
        b = block(a, dg, q)
        go(remote(b, b, i, 8, (sib, z)))

    total = 4 * count
    for t in range(total + 2):
        if t < total:
            stage0(t)
        if 0 <= t - 1 < total:
            stage1(t - 1)
        if 0 <= t - 2 < total:
            stage2(t - 2)
    for i in range(total):
        a, d = divmod(i, 4)
        q = q_of(d)
        for k, src in ((5, sib), (6, xn + dc), (7, yn + dc), (8, dg + dc)):
            b = block(a, src, q)
            remote(b, b, i, k, (sib, z)).wait_recv()
    if with_meta:
        for d in range(1, 8):
            metas[d - 1].wait()
    for c in local:
        c.wait()
    for c in sent:
        c.wait_send()


def gather(arrays, meta, collective_id):
    count = len(arrays)
    rows, cols = arrays[0].shape
    out = [jax.ShapeDtypeStruct((rows * 8, cols * 4), jnp.bfloat16)] * count
    args = list(arrays)
    if meta is not None:
        args.append(meta)
        out.append(jax.ShapeDtypeStruct((rows * 8, meta.shape[1]), jnp.bfloat16))
    return pl.pallas_call(
        functools.partial(gather_kernel, count, meta is not None),
        out_shape=out,
        in_specs=[VMEM] * len(args),
        out_specs=[HBM] * len(out),
        scratch_shapes=[
            pltpu.SemaphoreType.DMA((4 * count, 9)),
            pltpu.SemaphoreType.DMA((4 * count, 9)),
            pltpu.SemaphoreType.DMA((count + 1,)),
            pltpu.SemaphoreType.DMA((8,)),
            pltpu.SemaphoreType.DMA((8,)),
        ],
        compiler_params=pltpu.CompilerParams(
            collective_id=collective_id, has_side_effects=True, vmem_limit_bytes=GRANT
        ),
    )(*args)


def reduce_kernel(p_ref, out_ref, got_s, got_d, got_x, got_y, got_z, acc, send, recv):
    dp, z, dx, dy, dc = places()
    rows, cols = out_ref.shape
    half = rows // 2
    xn, yn, sib, dg = dp + dx, dp + dy, dp + dc, dp + dx + dy
    zs = [lax.rem(z + d, 4) for d in range(4)]
    meet(dp, z, [(dp, zs[d]) for d in (1, 2, 3)] + [(xn, z), (yn, z), (sib, z)])
    f32 = jnp.float32

    def p_at(q, owner, lo=0, n=rows):
        return p_ref.at[
            pl.ds(pl.multiple_of(owner * rows + lo, 16), n), pl.ds(pl.multiple_of(q * cols, 128), cols)
        ]

    def mine(q, owner, lo=0, n=rows):
        return p_at(q, owner, lo, n)[...].astype(f32)

    def remote(src, dst, i, kind, dev):
        return pltpu.make_async_remote_copy(
            src_ref=src, dst_ref=dst, send_sem=send.at[i, kind], recv_sem=recv.at[i, kind],
            device_id=dev, device_id_type=MESH,
        )

    sent = []

    def go(c):
        c.start()
        sent.append(c)

    lo, hi = pl.ds(0, half), pl.ds(half, half)
    order = [zs[2], zs[1], zs[3], zs[0]]
    slots = [(3, dg), (1, xn), (2, yn), (0, dp)]
    for i in range(4):
        q = order[i]
        for s, owner in slots:
            go(remote(p_at(q, owner + dc), got_s.at[q, s], i, s, (sib, z)))

    def arrive_s(i, s):
        remote(got_s.at[order[i], s], got_s.at[order[i], s], i, s, (sib, z)).wait_recv()

    def fold_diag(i):
        q = order[i]
        arrive_s(i, 3)
        acc[q, 3] = (mine(q, dg) + got_s[q, 3].astype(f32)).astype(jnp.bfloat16)
        go(remote(acc.at[q, 3, lo, :], got_d.at[q, 0], i, 4, (yn, z)))
        go(remote(acc.at[q, 3, hi, :], got_d.at[q, 1], i, 5, (xn, z)))

    def fold_side(i):
        q = order[i]
        arrive_s(i, 1)
        remote(got_d.at[q, 0], got_d.at[q, 0], i, 4, (yn, z)).wait_recv()
        acc[q, 1, lo, :] = (
            mine(q, xn, 0, half) + got_s[q, 1, lo, :].astype(f32) + got_d[q, 0].astype(f32)
        ).astype(jnp.bfloat16)
        acc[q, 1, hi, :] = (
            mine(q, xn, half, half) + got_s[q, 1, hi, :].astype(f32)
        ).astype(jnp.bfloat16)
        go(remote(acc.at[q, 1], got_x.at[q], i, 6, (xn, z)))
        arrive_s(i, 2)
        remote(got_d.at[q, 1], got_d.at[q, 1], i, 5, (xn, z)).wait_recv()
        acc[q, 2, hi, :] = (
            mine(q, yn, half, half) + got_s[q, 2, hi, :].astype(f32) + got_d[q, 1].astype(f32)
        ).astype(jnp.bfloat16)
        acc[q, 2, lo, :] = (
            mine(q, yn, 0, half) + got_s[q, 2, lo, :].astype(f32)
        ).astype(jnp.bfloat16)
        go(remote(acc.at[q, 2], got_y.at[q], i, 7, (yn, z)))

    def fold_own(i):
        q = order[i]
        arrive_s(i, 0)
        remote(got_x.at[q], got_x.at[q], i, 6, (xn, z)).wait_recv()
        remote(got_y.at[q], got_y.at[q], i, 7, (yn, z)).wait_recv()
        total = (
            mine(q, dp) + got_s[q, 0].astype(f32) + got_x[q].astype(f32) + got_y[q].astype(f32)
        )
        if i < 3:
            acc[q, 0] = total.astype(jnp.bfloat16)
            go(remote(acc.at[q, 0], got_z.at[i], i, 8, (dp, q)))
            return None
        for k in range(3):
            remote(got_z.at[k], got_z.at[k], k, 8, (dp, z)).wait_recv()
            total = total + got_z[k].astype(f32)
        out_ref[...] = total.astype(jnp.bfloat16)

    for t in range(6):
        if t < 4:
            fold_diag(t)
        if 0 <= t - 1 < 4:
            fold_side(t - 1)
        if 0 <= t - 2 < 4:
            fold_own(t - 2)
    for c in sent:
        c.wait_send()


def reduce_scatter(dense, rows, cols, collective_id):
    bf = jnp.bfloat16
    return pl.pallas_call(
        reduce_kernel,
        out_shape=jax.ShapeDtypeStruct((rows, cols), bf),
        in_specs=[VMEM],
        out_specs=VMEM,
        scratch_shapes=[
            pltpu.VMEM((4, 4, rows, cols), bf),
            pltpu.VMEM((4, 2, rows // 2, cols), bf),
            pltpu.VMEM((4, rows, cols), bf),
            pltpu.VMEM((4, rows, cols), bf),
            pltpu.VMEM((3, rows, cols), bf),
            pltpu.VMEM((4, 4, rows, cols), bf),
            pltpu.SemaphoreType.DMA((4, 9)),
            pltpu.SemaphoreType.DMA((4, 9)),
        ],
        compiler_params=pltpu.CompilerParams(
            collective_id=collective_id, has_side_effects=True, vmem_limit_bytes=GRANT
        ),
    )(dense)


CONTRACT = (((1,), (1,)), ((), ()))


def expert_rows(flat_x, flat_dy, gates, w_gate, w_up, w_down):
    f32 = jnp.float32
    gate_pre = jnp.dot(flat_x, w_gate, preferred_element_type=f32)
    up_pre = jnp.dot(flat_x, w_up, preferred_element_type=f32)
    scaled = gates * lax.dot_general(flat_dy, w_down, CONTRACT, preferred_element_type=f32)
    sigma = jax.nn.sigmoid(gate_pre)
    grad_gate = (scaled * up_pre * sigma * (1.0 + gate_pre * (1.0 - sigma))).astype(jnp.bfloat16)
    grad_up = (scaled * gate_pre * sigma).astype(jnp.bfloat16)
    part = lax.dot_general(grad_gate, w_gate, CONTRACT, preferred_element_type=f32)
    part = part + lax.dot_general(grad_up, w_up, CONTRACT, preferred_element_type=f32)
    return part.astype(jnp.bfloat16)


def on_device_block(tokens, cotangent, expert_ids, routing_weights, w_gate, w_up, w_down, embedding):
    f32, bf = jnp.float32, jnp.bfloat16
    rows, cols = tokens.shape
    count = rows * 8
    meta = jnp.concatenate(
        [expert_ids.astype(bf), routing_weights, jnp.zeros((rows, 128 - 2 * TOP), bf)], axis=1
    )
    all_x, all_dy, all_meta = gather([tokens, cotangent], meta, 1)
    mine = lax.axis_index("dp").astype(f32)
    named = all_meta[:, :TOP].astype(f32) == mine
    match = jnp.sum(named.astype(f32), axis=1)
    weight = jnp.sum(jnp.where(named, all_meta[:, TOP : 2 * TOP].astype(f32), 0.0), axis=1)
    row = jnp.arange(count, dtype=jnp.int32)
    earlier = (row[None, :] < row[:, None]).astype(bf)
    rank = jnp.dot(earlier, match.astype(bf)[:, None], preferred_element_type=f32)[:, 0].astype(jnp.int32)
    slot = jnp.arange(E * MOST, dtype=jnp.int32)
    chosen = (slot[:, None] == rank[None, :]) & (match[None, :] > 0.5)
    select = chosen.astype(bf)
    gates = jnp.sum(jnp.where(chosen, weight[None, :], 0.0), axis=1, keepdims=True)
    flat_x = jnp.dot(select, all_x, preferred_element_type=f32).astype(bf)
    flat_dy = jnp.dot(select, all_dy, preferred_element_type=f32).astype(bf)
    part = expert_rows(flat_x, flat_dy, gates, w_gate, w_up, w_down)
    dense = lax.dot_general(select, part, (((0,), (0,)), ((), ())), preferred_element_type=f32).astype(bf)
    input_grad = reduce_scatter(dense, rows, cols, 2)
    (whole,) = gather([input_grad], None, 3)
    scores = -lax.dot_general(whole, embedding, CONTRACT, preferred_element_type=f32)
    return input_grad, scores


def owner_work(rows_x, rows_dy, gates, w_gate, w_up, w_down):
    sources, slots, width = rows_x.shape
    part = expert_rows(
        rows_x.reshape(sources * slots, width),
        rows_dy.reshape(sources * slots, width),
        gates.reshape(sources * slots, 1).astype(jnp.float32),
        w_gate,
        w_up,
        w_down,
    )
    return part.reshape(sources, slots, width)


def on_device_any(tokens, cotangent, expert_ids, routing_weights, w_gate, w_up, w_down, embedding):
    dp_count = lax.axis_size("dp")
    owners = dp_count // E
    tok_rows = tokens.shape[0]
    pair_count = tok_rows * TOP
    flat_ids = expert_ids.reshape(pair_count)
    expert_iota = jnp.arange(E, dtype=jnp.int32)
    onehot = (flat_ids[:, None] == expert_iota[None, :]).astype(jnp.float32)
    pair_iota = jnp.arange(pair_count, dtype=jnp.int32)
    earlier = (pair_iota[:, None] > pair_iota[None, :]).astype(jnp.float32)
    before = jnp.dot(earlier, onehot, precision=lax.Precision.HIGHEST)
    slot_rank = jnp.sum(before * onehot, axis=1).astype(jnp.int32)
    slot_of = flat_ids * MOST + slot_rank
    slot_iota = jnp.arange(E * MOST, dtype=jnp.int32)
    placed = slot_iota[:, None] == slot_of[None, :]
    flat_weights = routing_weights.reshape(pair_count).astype(jnp.float32)
    gate_slots = jnp.sum(jnp.where(placed, flat_weights[None, :], 0.0), axis=1).astype(jnp.bfloat16)
    select_rows = jnp.sum(
        placed.reshape(E * MOST, tok_rows, TOP).astype(jnp.float32), axis=2
    ).astype(jnp.bfloat16)
    send_gates = jnp.repeat(gate_slots.reshape(E, MOST), owners, axis=0)

    def dispatch(rows):
        packed = jnp.dot(select_rows, rows, preferred_element_type=jnp.float32).astype(jnp.bfloat16)
        return jnp.repeat(packed.reshape(E, MOST, rows.shape[1]), owners, axis=0)

    whole_x, whole_dy = (
        lax.all_gather(tokens, "expert", axis=1, tiled=True),
        lax.all_gather(cotangent, "expert", axis=1, tiled=True),
    )
    recv_x, recv_dy, recv_gates = (
        lax.all_to_all(dispatch(whole_x), "dp", split_axis=0, concat_axis=0, tiled=True),
        lax.all_to_all(dispatch(whole_dy), "dp", split_axis=0, concat_axis=0, tiled=True),
        lax.all_to_all(send_gates, "dp", split_axis=0, concat_axis=0, tiled=True),
    )
    partial_rows = owner_work(recv_x, recv_dy, recv_gates, w_gate, w_up, w_down)
    came_back = lax.all_to_all(partial_rows, "dp", split_axis=0, concat_axis=0, tiled=True)
    returned = lax.psum_scatter(
        came_back.astype(jnp.float32).astype(jnp.bfloat16),
        "expert",
        scatter_dimension=2,
        tiled=True,
    )
    spread = jnp.repeat(select_rows.reshape(E, MOST, tok_rows), owners, axis=0).reshape(
        dp_count * MOST, tok_rows
    )
    feature_count = returned.shape[2]
    input_grad = lax.dot_general(
        spread,
        returned.reshape(dp_count * MOST, feature_count),
        (((0,), (0,)), ((), ())),
        preferred_element_type=jnp.float32,
    ).astype(jnp.bfloat16)
    whole_grad = lax.all_gather(input_grad, "expert", axis=1, tiled=True)
    scores = -lax.dot_general(
        lax.all_gather(whole_grad, "dp", axis=0, tiled=True),
        embedding,
        (((1,), (1,)), ((), ())),
        preferred_element_type=jnp.float32,
    )
    return (input_grad, scores)


def solution(mesh):
    placed = (
        P("dp", "expert"),
        P("dp", "expert"),
        P("dp", None),
        P("dp", None),
        P(None, ("dp", "expert")),
        P(None, ("dp", "expert")),
        P(("dp", "expert"), None),
        P(("dp", "expert"), None),
    )
    block = mesh.shape["dp"] == 8 and mesh.shape["expert"] == 4
    return jax.shard_map(
        on_device_block if block else on_device_any,
        mesh=mesh,
        in_specs=placed,
        out_specs=(P("dp", "expert"), P(None, ("dp", "expert"))),
        check_vma=False,
    )
```
